32 devices in a mesh: dp: 8 (over z, x), head: 4 (over y, core).
Axes of the slice: x: 2, y: 2, z: 4, core: 2. Of those that a mesh axis runs over, the one named last changes fastest.
Arguments:
- vit_ctx: bfloat16 [1024, 1536], P('dp', 'head'), may hold values from -6 to 6
- vit_resid: bfloat16 [1024, 1600], P('dp'), may hold values from -6 to 6
- vit_proj: bfloat16 [4, 384, 1600], P('head', 'dp'), may hold values from -0.15625 to 0.15625
- vit_grad: bfloat16 [1024, 1600], P('dp'), may hold values from -6 to 6
- norm_gain: float32 [1600], replicated, may hold values from 0.1 to 1.9
- cross_q: bfloat16 [96, 2048], P(None, 'head'), may hold values from -400 to 400
- key_w: bfloat16 [1600, 2048], P(None, 'head'), may hold values from -0.15625 to 0.15625
- value_w: bfloat16 [1600, 2048], P(None, 'head'), may hold values from -0.15625 to 0.15625
- out_w: bfloat16 [2048, 4096], P('head'), may hold values from -0.125 to 0.125
- query_state: bfloat16 [96, 4096], P(None, 'head'), may hold values from -1.5 to 1.5
Outputs:
- ctx_grad: bfloat16 [1024, 1536], P('dp', 'head')
- proj_grad: float32 [4, 384, 1600], P('head', 'dp')
- cross_out: bfloat16 [8, 96, 4096], P('dp', None, 'head')
The draws below stay inside these ranges and needn't reach their ends.
All inputs are finite; a program needn't handle non-finite values.
Results may differ from the reference program's by a relative error of at most 0.017.
The reference program's roundings to bfloat16 on the way count: a program that leaves them out, or rounds other values in their place, can miss the bound.
Values may be sent and summed in bfloat16 or wider, within the bound.
A program may use at most 64 MiB of HBM per device.

```python
import math
import jax
import jax.numpy as jnp
from jax import lax

D = 1600
HD = 128
QW = 4096
NQ = 96
TOK_DEV = 128
VROWS = 384
VCTX = 1536
CHEADS = 16
CW = 2048
VTOK = 1024
N_DP = 8
N_HEAD = 4


def draw_cross_q(key, part):
    base_key = jax.random.fold_in(jax.random.fold_in(key, 17), 0)
    values = jax.random.normal(base_key, (NQ, CHEADS * HD), jnp.float32)
    return jnp.clip(values, -400.0, 400.0).astype(jnp.bfloat16)


def levels(rng, shape, shards, smallest, high):
    gain, own = 1.0, jax.random.fold_in(rng, 6)
    for axis_at, parts in shards:
        steps = jnp.exp(jax.random.uniform(jax.random.fold_in(own, axis_at), (parts,), jnp.float32, smallest / len(shards), high / len(shards)))
        gain = gain * jnp.repeat(steps, shape[axis_at] // parts).reshape([-1 if axis == axis_at else 1 for axis in range(len(shape))])
    return gain


def noise(rng, dims, scale, most, pieces=(), kind=jnp.bfloat16):
    gain = levels(rng, dims, pieces, -0.22, 0.18) if pieces else 1.0
    values = jax.random.normal(rng, dims, jnp.float32) * scale * gain
    return jnp.minimum(jnp.maximum(values, -most), most).astype(kind)


def setup_inputs(seed: int = 0) -> dict:
    key_list = jax.random.split(jax.random.key(seed), 11)
    return {
        "vit_ctx": noise(key_list[0], (VTOK, VCTX), 1.0, 6.0, ((0, 8), (1, 4))),
        "vit_resid": noise(key_list[1], (VTOK, D), 1.0, 6.0, ((0, 8),)),
        "vit_proj": noise(key_list[2], (N_HEAD, VROWS, D), VCTX ** -0.5, 0.15625, ((0, 4), (1, 8))),
        "vit_grad": noise(key_list[3], (VTOK, D), 1.0, 6.0, ((0, 8),)),
        "norm_gain": jnp.clip(1.0 + 0.18 * jax.random.normal(key_list[4], (D,), jnp.float32), 0.1, 1.9),
        "cross_q": draw_cross_q(jax.random.fold_in(key_list[10], 71), 0),
        "key_w": noise(key_list[6], (D, CW), D ** -0.5, 0.15625, ((1, 4),)),
        "value_w": noise(key_list[7], (D, CW), D ** -0.5, 0.15625, ((1, 4),)),
        "out_w": noise(key_list[8], (CW, QW), CW ** -0.5, 0.125, ((0, 4),)),
        "query_state": noise(key_list[9], (NQ, QW), 0.25, 1.5, ((1, 4),)),
    }


EPSILON = 1e-06

def layer_norm(hidden, norm_gain):
    row_mean = lax.optimization_barrier(jnp.mean(hidden, axis=1, keepdims=True))
    square_mean = lax.optimization_barrier(jnp.mean(hidden * hidden, axis=1, keepdims=True))
    variance = square_mean - row_mean * row_mean
    return (hidden - row_mean) * lax.rsqrt(variance + EPSILON) * norm_gain

def reference(vit_ctx, vit_resid, vit_proj, vit_grad, norm_gain, cross_q, key_w, value_w, out_w, query_state):
    proj_matrix = vit_proj.reshape(VCTX, D)
    hidden = vit_resid.astype(jnp.float32) + jnp.dot(vit_ctx, proj_matrix, preferred_element_type=jnp.float32)
    features = layer_norm(hidden, norm_gain).astype(jnp.bfloat16)
    queries = cross_q.astype(jnp.float32).reshape(NQ, CHEADS, HD)

    def one_image(feats_image):
        key_rows = jnp.dot(feats_image, key_w, preferred_element_type=jnp.float32).astype(jnp.bfloat16)
        value_rows = jnp.dot(feats_image, value_w, preferred_element_type=jnp.float32).astype(jnp.bfloat16)
        key_heads = key_rows.astype(jnp.float32).reshape(TOK_DEV, CHEADS, HD)
        value_heads = value_rows.astype(jnp.float32).reshape(TOK_DEV, CHEADS, HD)
        scores = jnp.einsum('qhd,khd->hqk', queries, key_heads) * (1.0 / math.sqrt(HD))
        row_max = lax.optimization_barrier(jnp.max(scores, axis=2, keepdims=True))
        exponent = jnp.exp(scores - row_max)
        attn_probs = (exponent / lax.optimization_barrier(jnp.sum(exponent, axis=2, keepdims=True))).astype(jnp.bfloat16)
        attended = jnp.einsum('hqk,khd->qhd', attn_probs.astype(jnp.float32), value_heads)
        attended = attended.astype(jnp.bfloat16).reshape(NQ, CW)
        return (jnp.dot(attended, out_w, preferred_element_type=jnp.float32) + query_state.astype(jnp.float32)).astype(jnp.bfloat16)
    cross_out = lax.map(one_image, features.reshape(N_DP, TOK_DEV, D))
    ctx_grad = lax.dot_general(vit_grad, proj_matrix, (((1,), (1,)), ((), ())), preferred_element_type=jnp.float32).astype(jnp.bfloat16)
    proj_grad = lax.dot_general(vit_ctx, vit_grad, (((0,), (0,)), ((), ())), preferred_element_type=jnp.float32)
    return (ctx_grad, proj_grad.reshape(N_HEAD, VROWS, D), cross_out)
```

```python
import functools
import math

import jax
import jax.numpy as jnp
from jax import lax
from jax.experimental import pallas as pl
from jax.experimental.pallas import tpu as pltpu
from jax.sharding import PartitionSpec as P

HD = 128
EPSILON = 1e-06
MESH = pl.DeviceIdType.MESH
F32 = jnp.float32
BF16 = jnp.bfloat16


def peer_along(at, step, count):
    if count & (count - 1):
        return lax.rem(at + step, count)
    bit = 1
    while bit < count:
        if step & bit:
            at = at + bit - 2 * bit * lax.rem(at // bit, 2)
        bit *= 2
    return at


def kernel(names, n, h, fused, *refs):
    r = dict(zip(names, refs))
    ctx, resid, proj, grad, gain, cross_q, query_state = (
        r[k] for k in ("ctx", "resid", "proj", "grad", "gain", "cross_q", "query_state")
    )
    d, e = lax.axis_index("dp"), lax.axis_index("head")
    m, chips = n // 2, h // 2
    z, x = d // 2, lax.rem(d, 2)
    y, c = e // 2, lax.rem(e, 2)
    x_peer = (2 * z + 1 - x, e)
    z_pos = [z] + [peer_along(z, k, m) for k in range(1, m)] if fused else []
    z_peer = [(2 * p + x, e) for p in z_pos]
    core_peer = (d, 2 * y + 1 - c)
    y_pos = [y] + [lax.rem(y + k, chips) for k in range(1, chips)]
    y_peer = [(d, 2 * p + c) for p in y_pos]

    def remote(src, dst, name, at, device):
        copy = pltpu.make_async_remote_copy(
            src_ref=src,
            dst_ref=dst,
            send_sem=r[name + "_s"].at[at],
            recv_sem=r[name + "_r"].at[at],
            device_id=device,
            device_id_type=MESH,
        )
        copy.start()
        return copy

    loads = []
    for i, name in enumerate(("key_w", "value_w", "out_w")):
        load = pltpu.make_async_copy(r[name], r[name + "_v"], r["load"].at[i])
        load.start()
        loads.append(load)

    greet = ([x_peer] + z_peer[1:] if fused else []) + [core_peer] + y_peer[1:]
    barrier = pltpu.get_barrier_semaphore()
    for device in greet:
        pl.semaphore_signal(barrier, inc=1, device_id=device, device_id_type=MESH)
    pl.semaphore_wait(barrier, len(greet))

    if fused:
        rows = proj.shape[0]
        width = proj.shape[1]
        gath, dwf, dwb = r["gath"], r["dwf"], r["dwb"]
        ag_z = [None] + [remote(proj, gath.at[d], "ag_z", k - 1, z_peer[k]) for k in range(1, m)]
        ag_x = [remote(proj, gath.at[d], "ag_x", 0, x_peer)]
        gath[d] = proj[...]
        ctx_t = ctx[...].T
        for lo in range(0, width, 256):
            hi = min(lo + 256, width)
            part = jnp.dot(ctx_t, grad[:, lo:hi], preferred_element_type=F32)
            dwf[:, :, lo:hi] = part.reshape(n, rows, hi - lo)
        for k in range(m):
            dwb[k] = dwf[2 * z_pos[k] + 1 - x].astype(BF16)
        for k in range(1, m):
            ag_z[k].wait_recv()
            owner = 2 * z_pos[k] + x
            ag_x.append(remote(gath.at[owner], gath.at[owner], "ag_x", k, x_peer))
        rs_x = {}
        for k in list(range(m - 1, 0, -1)) + [0]:
            rs_x[k] = remote(dwb.at[k], r["xrecv"].at[k], "rs_x", k, x_peer)
        rs_z = {}

        def pass_on(k):
            rs_x[k].wait_recv()
            r["zsend"][k - 1] = (dwf[2 * z_pos[k] + x] + r["xrecv"][k].astype(F32)).astype(BF16)
            rs_z[k] = remote(r["zsend"].at[k - 1], r["zrecv"].at[k - 1], "rs_z", k - 1, z_peer[k])

        for k in range(m):
            ag_x[k].wait_recv()
        matrix = gath[...].reshape(n * rows, width)
        todo = list(range(m - 1, 0, -1))
    else:
        matrix = proj[...]
        todo = []

    half = ctx.shape[0] // 2
    own_rows = pl.ds(pl.multiple_of(c * half, half), half)
    peer_rows = pl.ds(pl.multiple_of((1 - c) * half, half), half)
    hs, feat = r["hs"], r["feat"]
    hs[1] = jnp.dot(ctx[peer_rows, :], matrix, preferred_element_type=F32)
    to_core = remote(hs.at[1], r["crecv"], "core", 0, core_peer)
    hs[0] = jnp.dot(ctx[own_rows, :], matrix, preferred_element_type=F32)
    to_core.wait_recv()
    chip_sum = hs[0] + r["crecv"][...]
    hs[0] = chip_sum
    r["ysend"][...] = chip_sum.astype(BF16)
    to_y = [remote(r["ysend"], r["yrecv"].at[k - 1], "y", k - 1, y_peer[k]) for k in range(1, chips)]

    r["ctx_grad"][...] = lax.dot_general(
        grad[...], matrix, (((1,), (1,)), ((), ())), preferred_element_type=F32
    ).astype(BF16)
    if todo:
        pass_on(todo.pop(0))

    hidden = resid[own_rows, :].astype(F32) + hs[0]
    for k in range(1, chips):
        to_y[k - 1].wait_recv()
        hidden = hidden + r["yrecv"][k - 1].astype(F32)
    features = hidden.shape[1]
    row_mean = jnp.sum(hidden, axis=1, keepdims=True) / features
    square_mean = jnp.sum(hidden * hidden, axis=1, keepdims=True) / features
    variance = square_mean - row_mean * row_mean
    feat[own_rows, :] = (
        (hidden - row_mean) * lax.rsqrt(variance + EPSILON) * gain[...]
    ).astype(BF16)
    to_feat = remote(feat.at[own_rows], feat.at[own_rows], "feat", 0, core_peer)
    if len(todo) > 1:
        pass_on(todo.pop(0))
    loads[0].wait()
    loads[1].wait()
    to_feat.wait_recv()

    rows_of = feat[...]
    keys = jnp.dot(rows_of, r["key_w_v"][...], preferred_element_type=F32).astype(BF16)
    values = jnp.dot(rows_of, r["value_w_v"][...], preferred_element_type=F32).astype(BF16)
    scale = 1.0 / math.sqrt(HD)
    attended = []
    for lo in range(0, keys.shape[1], HD):
        scores = (
            lax.dot_general(
                cross_q[:, lo : lo + HD],
                keys[:, lo : lo + HD],
                (((1,), (1,)), ((), ())),
                preferred_element_type=F32,
            )
            * scale
        )
        exponent = jnp.exp(scores - jnp.max(scores, axis=1, keepdims=True))
        probs = (exponent / jnp.sum(exponent, axis=1, keepdims=True)).astype(BF16)
        attended.append(
            jnp.dot(probs, values[:, lo : lo + HD], preferred_element_type=F32).astype(BF16)
        )
    attended = jnp.concatenate(attended, axis=1)

    loads[2].wait()
    out_w, wide = r["out_w_v"], query_state.shape[1]

    def term(chip, core):
        at = pl.multiple_of((2 * chip + core) * wide, 128)
        return jnp.dot(attended, out_w[:, pl.ds(at, wide)], preferred_element_type=F32)

    osend, orecv, own = r["osend"], r["orecv"], r["own"]
    to_pair, to_out = {}, {}
    order = list(range(1, chips)) + [0]
    for k in order:
        osend[k] = term(y_pos[k], 1 - c).astype(BF16)
        to_pair[k] = remote(osend.at[k], orecv.at[k], "pair", k, core_peer)
        own[k] = term(y_pos[k], c)
        if k:
            to_pair[k].wait_recv()
            r["o2send"][k - 1] = (own[k] + orecv[k].astype(F32)).astype(BF16)
            to_out[k] = remote(r["o2send"].at[k - 1], r["o2recv"].at[k - 1], "out", k - 1, y_peer[k])

    while todo:
        pass_on(todo.pop(0))
    if fused:
        rs_x[0].wait_recv()
        total = dwf[d] + r["xrecv"][0].astype(F32)
        for k in range(m - 1, 0, -1):
            rs_z[k].wait_recv()
            total = total + r["zrecv"][k - 1].astype(F32)
        r["proj_grad"][...] = total

    to_pair[0].wait_recv()
    result = query_state[...].astype(F32) + own[0] + orecv[0].astype(F32)
    for k in range(1, chips):
        to_out[k].wait_recv()
        result = result + r["o2recv"][k - 1].astype(F32)
    r["cross_out"][...] = result.astype(BF16)

    sends = [to_core, to_feat] + to_y + list(to_pair.values()) + list(to_out.values())
    if fused:
        sends += ag_z[1:] + ag_x + list(rs_x.values()) + list(rs_z.values())
    for copy in sends:
        copy.wait_send()


def on_device(
    n, h, vit_ctx, vit_resid, vit_proj, vit_grad, norm_gain, cross_q, key_w, value_w, out_w, query_state
):
    rows, width = vit_proj.shape[1:]
    fused = rows % 16 == 0 and n % 2 == 0
    tokens, vrows = vit_ctx.shape
    queries, wide = query_state.shape
    m, chips, half = n // 2, h // 2, tokens // 2
    proj = vit_proj[0] if fused else lax.all_gather(vit_proj, "dp", axis=1, tiled=True)[0]

    ins = {
        "ctx": vit_ctx, "resid": vit_resid, "proj": proj, "grad": vit_grad,
        "gain": norm_gain[None], "cross_q": cross_q, "query_state": query_state,
    }
    streamed = {"key_w": key_w, "value_w": value_w, "out_w": out_w}
    outs = {"ctx_grad": ((tokens, vrows), BF16), "cross_out": ((queries, wide), BF16)}
    dma = lambda count: pltpu.SemaphoreType.DMA((max(count, 1),))
    scratch = {name + "_v": pltpu.VMEM(a.shape, a.dtype) for name, a in streamed.items()}
    scratch |= {
        "load": dma(3),
        "hs": pltpu.VMEM((2, half, width), F32),
        "crecv": pltpu.VMEM((half, width), F32),
        "ysend": pltpu.VMEM((half, width), BF16),
        "yrecv": pltpu.VMEM((max(chips - 1, 1), half, width), BF16),
        "feat": pltpu.VMEM((tokens, width), BF16),
        "osend": pltpu.VMEM((chips, queries, wide), BF16),
        "orecv": pltpu.VMEM((chips, queries, wide), BF16),
        "own": pltpu.VMEM((chips, queries, wide), F32),
        "o2send": pltpu.VMEM((max(chips - 1, 1), queries, wide), BF16),
        "o2recv": pltpu.VMEM((max(chips - 1, 1), queries, wide), BF16),
    }
    sems = {"core": 1, "y": chips - 1, "feat": 1, "pair": chips, "out": chips - 1}
    if fused:
        outs["proj_grad"] = ((rows, width), F32)
        scratch |= {
            "gath": pltpu.VMEM((n, rows, width), BF16),
            "dwf": pltpu.VMEM((n, rows, width), F32),
            "dwb": pltpu.VMEM((m, rows, width), BF16),
            "xrecv": pltpu.VMEM((m, rows, width), BF16),
            "zsend": pltpu.VMEM((max(m - 1, 1), rows, width), BF16),
            "zrecv": pltpu.VMEM((max(m - 1, 1), rows, width), BF16),
        }
        sems |= {"ag_z": m - 1, "ag_x": m, "rs_x": m, "rs_z": m - 1}
    for name, count in sems.items():
        scratch |= {name + "_s": dma(count), name + "_r": dma(count)}

    names = list(ins) + list(streamed) + list(outs) + list(scratch)
    vmem = pl.BlockSpec(memory_space=pltpu.VMEM)
    results = pl.pallas_call(
        functools.partial(kernel, names, n, h, fused),
        out_shape=[jax.ShapeDtypeStruct(*v) for v in outs.values()],
        in_specs=[vmem] * len(ins) + [pl.BlockSpec(memory_space=pl.ANY)] * len(streamed),
        out_specs=[vmem] * len(outs),
        scratch_shapes=list(scratch.values()),
        compiler_params=pltpu.CompilerParams(collective_id=0, has_side_effects=True),
    )(*ins.values(), *streamed.values())
    results = dict(zip(outs, results))
    if fused:
        proj_grad = results["proj_grad"]
    else:
        proj_grad = lax.psum_scatter(
            lax.dot_general(vit_ctx, vit_grad, (((0,), (0,)), ((), ())), preferred_element_type=F32),
            "dp", scatter_dimension=0, tiled=True,
        )
    return (results["ctx_grad"], proj_grad[None], results["cross_out"][None])


def solution(mesh):
    return jax.shard_map(
        functools.partial(on_device, mesh.shape["dp"], mesh.shape["head"]),
        mesh=mesh,
        in_specs=(
            P("dp", "head"),
            P("dp", None),
            P("head", "dp", None),
            P("dp", None),
            P(),
            P(None, "head"),
            P(None, "head"),
            P(None, "head"),
            P("head", None),
            P(None, "head"),
        ),
        out_specs=(P("dp", "head"), P("head", "dp", None), P("dp", None, "head")),
        check_vma=False,
    )
```

```python
import functools
import math

import jax
import jax.numpy as jnp
from jax import lax
from jax.experimental import pallas as pl
from jax.experimental.pallas import tpu as pltpu
from jax.sharding import PartitionSpec as P

HD = 128
EPSILON = 1e-06
MESH = pl.DeviceIdType.MESH
F32 = jnp.float32
BF16 = jnp.bfloat16


def peer_along(at, step, count):
    if count & (count - 1):
        return lax.rem(at + step, count)
    bit = 1
    while bit < count:
        if step & bit:
            at = at + bit - 2 * bit * lax.rem(at // bit, 2)
        bit *= 2
    return at


def kernel(names, n, h, fused, spans, *refs):
    r = dict(zip(names, refs), spans=spans)
    ctx, resid, proj, grad, gain, cross_q, query_state = (
        r[k] for k in ("ctx", "resid", "proj", "grad", "gain", "cross_q", "query_state")
    )
    d, e = lax.axis_index("dp"), lax.axis_index("head")
    m, chips = n // 2, h // 2
    z, x = d // 2, lax.rem(d, 2)
    y, c = e // 2, lax.rem(e, 2)
    x_peer = (2 * z + 1 - x, e)
    z_pos = [z] + [peer_along(z, k, m) for k in range(1, m)] if fused else []
    z_peer = [(2 * p + x, e) for p in z_pos]
    core_peer = (d, 2 * y + 1 - c)
    y_pos = [y] + [lax.rem(y + k, chips) for k in range(1, chips)]
    y_peer = [(d, 2 * p + c) for p in y_pos]

    def remote(src, dst, name, at, device):
        copy = pltpu.make_async_remote_copy(
            src_ref=src,
            dst_ref=dst,
            send_sem=r[name + "_s"].at[at],
            recv_sem=r[name + "_r"].at[at],
            device_id=device,
            device_id_type=MESH,
        )
        copy.start()
        return copy

    loads = []
    for i, name in enumerate(("key_w", "value_w", "out_w")):
        load = pltpu.make_async_copy(r[name], r[name + "_v"], r["load"].at[i])
        load.start()
        loads.append(load)

    greet = ([x_peer] + z_peer[1:] if fused else []) + [core_peer] + y_peer[1:]
    barrier = pltpu.get_barrier_semaphore()
    for device in greet:
        pl.semaphore_signal(barrier, inc=1, device_id=device, device_id_type=MESH)
    pl.semaphore_wait(barrier, len(greet))

    spans = r["spans"]
    width = spans[-1][1]

    def flip(src, dst):
        for lo in range(0, width, 128):
            hi = min(lo + 128, width)
            dst[:, lo:hi] = src[lo:hi, :].T

    if fused:
        rows = proj.shape[0]
        dwf, dwb = r["dwf"], r["dwb"]
        ag_z, ag_x = {}, {}
        for i, (lo, hi) in enumerate(spans):
            piece, gath = proj.at[:, lo:hi], r[f"gath{i}"]
            ag_x[i, 0] = remote(piece, gath.at[d], f"ag_x{i}", 0, x_peer)
            for k in range(1, m):
                ag_z[i, k] = remote(piece, gath.at[d], f"ag_z{i}", k - 1, z_peer[k])
            gath[d] = piece[...]
        ctx_t = ctx[...].T
        for lo in range(0, width, 256):
            hi = min(lo + 256, width)
            part = lax.dot_general(
                ctx_t, grad[lo:hi, :], (((1,), (1,)), ((), ())), preferred_element_type=F32
            )
            dwf[:, :, lo:hi] = part.reshape(n, rows, hi - lo)
        for k in range(m):
            dwb[k] = dwf[2 * z_pos[k] + 1 - x].astype(BF16)
    flip(grad, r["grad_n"])
    flip(resid, r["resid_n"])
    grad, resid = r["grad_n"], r["resid_n"]

    half = ctx.shape[0] // 2
    own_rows = pl.ds(pl.multiple_of(c * half, half), half)
    peer_rows = pl.ds(pl.multiple_of((1 - c) * half, half), half)
    feat = r["feat"]
    to_core, to_y, rs_x, rs_z = {}, {}, {}, {}

    def forward(i, k):
        ag_z[i, k].wait_recv()
        here = r[f"gath{i}"].at[2 * z_pos[k] + x]
        ag_x[i, k] = remote(here, here, f"ag_x{i}", k, x_peer)

    def matrix(i):
        lo, hi = spans[i]
        return r[f"gath{i}"][...].reshape(n * rows, hi - lo) if fused else proj[:, lo:hi]

    def product(i):
        if fused:
            for k in range(m):
                ag_x[i, k].wait_recv()
        hs = r[f"hs{i}"]
        hs[1] = jnp.dot(ctx[peer_rows, :], matrix(i), preferred_element_type=F32)
        to_core[i] = remote(hs.at[1], r[f"crecv{i}"], f"core{i}", 0, core_peer)
        hs[0] = jnp.dot(ctx[own_rows, :], matrix(i), preferred_element_type=F32)

    def exchange(i):
        hs, ysend, yrecv = r[f"hs{i}"], r[f"ysend{i}"], r[f"yrecv{i}"]
        to_core[i].wait_recv()
        chip_sum = hs[0] + r[f"crecv{i}"][...]
        hs[0] = chip_sum
        ysend[...] = chip_sum.astype(BF16)
        for k in range(1, chips):
            to_y[i, k] = remote(ysend, yrecv.at[k - 1], f"y{i}", k - 1, y_peer[k])

    def pass_on(k):
        rs_x[k].wait_recv()
        r["zsend"][k - 1] = (dwf[2 * z_pos[k] + x] + r["xrecv"][k].astype(F32)).astype(BF16)
        rs_z[k] = remote(r["zsend"].at[k - 1], r["zrecv"].at[k - 1], "rs_z", k - 1, z_peer[k])

    todo = list(range(m - 1, 0, -1)) if fused else []
    last = len(spans) - 1
    for i in range(len(spans)):
        steps = list(range(1, m)) if fused else []
        if i == 0:
            for k in steps:
                forward(i, k)
        ahead = steps if i < last else []
        for k in ahead[:1]:
            forward(i + 1, k)
        product(i)
        for k in ahead[1:2]:
            forward(i + 1, k)
        exchange(i)
        for k in ahead[2:]:
            forward(i + 1, k)
        if fused and i == max(last - 1, 0):
            for k in todo + [0]:
                rs_x[k] = remote(dwb.at[k], r["xrecv"].at[k], "rs_x", k, x_peer)

    grads = 0.0
    for i, (lo, hi) in enumerate(spans):
        grads = grads + lax.dot_general(
            grad[:, lo:hi], matrix(i), (((1,), (1,)), ((), ())), preferred_element_type=F32
        )
    r["ctx_grad"][...] = grads.astype(BF16)
    if todo:
        pass_on(todo.pop(0))

    total, squares = 0.0, 0.0
    for i, (lo, hi) in enumerate(spans):
        hidden = resid[own_rows, lo:hi].astype(F32) + r[f"hs{i}"][0]
        for k in range(1, chips):
            to_y[i, k].wait_recv()
            hidden = hidden + r[f"yrecv{i}"][k - 1].astype(F32)
        r[f"hs{i}"][0] = hidden
        total = total + jnp.sum(hidden, axis=1, keepdims=True)
        squares = squares + jnp.sum(hidden * hidden, axis=1, keepdims=True)
    row_mean, square_mean = total / width, squares / width
    variance = square_mean - row_mean * row_mean
    inverse = lax.rsqrt(variance + EPSILON)
    scales = gain[...].reshape(1, width)
    for i, (lo, hi) in enumerate(spans):
        feat[own_rows, lo:hi] = (
            (r[f"hs{i}"][0] - row_mean) * inverse * scales[:, lo:hi]
        ).astype(BF16)
    to_feat = remote(feat.at[own_rows], feat.at[own_rows], "feat", 0, core_peer)
    if len(todo) > 1:
        pass_on(todo.pop(0))
    loads[0].wait()
    loads[1].wait()
    to_feat.wait_recv()

    rows_of = feat[...]
    keys = jnp.dot(rows_of, r["key_w_v"][...], preferred_element_type=F32).astype(BF16)
    values = jnp.dot(rows_of, r["value_w_v"][...], preferred_element_type=F32).astype(BF16)
    scale = 1.0 / math.sqrt(HD)
    attended = []
    for lo in range(0, keys.shape[1], HD):
        scores = (
            lax.dot_general(
                cross_q[:, lo : lo + HD],
                keys[:, lo : lo + HD],
                (((1,), (1,)), ((), ())),
                preferred_element_type=F32,
            )
            * scale
        )
        exponent = jnp.exp(scores - jnp.max(scores, axis=1, keepdims=True))
        probs = (exponent / jnp.sum(exponent, axis=1, keepdims=True)).astype(BF16)
        attended.append(
            jnp.dot(probs, values[:, lo : lo + HD], preferred_element_type=F32).astype(BF16)
        )
    attended = jnp.concatenate(attended, axis=1)

    loads[2].wait()
    out_w, wide = r["out_w_v"], query_state.shape[1]

    def term(chip, core):
        at = pl.multiple_of((2 * chip + core) * wide, 128)
        return jnp.dot(attended, out_w[:, pl.ds(at, wide)], preferred_element_type=F32)

    osend, orecv, own = r["osend"], r["orecv"], r["own"]
    to_pair, to_out = {}, {}
    order = list(range(1, chips)) + [0]
    for k in order:
        osend[k] = term(y_pos[k], 1 - c).astype(BF16)
        to_pair[k] = remote(osend.at[k], orecv.at[k], "pair", k, core_peer)
        own[k] = term(y_pos[k], c)
        if k:
            to_pair[k].wait_recv()
            r["o2send"][k - 1] = (own[k] + orecv[k].astype(F32)).astype(BF16)
            to_out[k] = remote(r["o2send"].at[k - 1], r["o2recv"].at[k - 1], "out", k - 1, y_peer[k])

    while todo:
        pass_on(todo.pop(0))
    if fused:
        rs_x[0].wait_recv()
        total = dwf[d] + r["xrecv"][0].astype(F32)
        for k in range(m - 1, 0, -1):
            rs_z[k].wait_recv()
            total = total + r["zrecv"][k - 1].astype(F32)
        r["proj_grad"][...] = total

    to_pair[0].wait_recv()
    result = query_state[...].astype(F32) + own[0] + orecv[0].astype(F32)
    for k in range(1, chips):
        to_out[k].wait_recv()
        result = result + r["o2recv"][k - 1].astype(F32)
    r["cross_out"][...] = result.astype(BF16)

    groups = [to_core, to_y, to_pair, to_out] + ([ag_z, ag_x, rs_x, rs_z] if fused else [])
    sends = [to_feat] + [copy for group in groups for copy in group.values()]
    for copy in sends:
        copy.wait_send()


def hand_over(*refs):
    count = len(refs) // 2
    for src, dst in zip(refs[:count], refs[count:]):
        dst[...] = src[...]


def on_device(
    n, h, vit_ctx, vit_resid, vit_proj, vit_grad, norm_gain, cross_q, key_w, value_w, out_w, query_state
):
    rows, width = vit_proj.shape[1:]
    fused = rows % 16 == 0 and n % 2 == 0
    tokens, vrows = vit_ctx.shape
    queries, wide = query_state.shape
    m, chips, half = n // 2, h // 2, tokens // 2
    proj = vit_proj[0] if fused else lax.all_gather(vit_proj, "dp", axis=1, tiled=True)[0]

    ins = {
        "ctx": vit_ctx, "resid": vit_resid.T, "proj": proj, "grad": vit_grad.T,
        "gain": norm_gain, "cross_q": cross_q, "query_state": query_state,
    }
    streamed = {"key_w": key_w, "value_w": value_w, "out_w": out_w}
    outs = {"ctx_grad": ((tokens, vrows), BF16), "cross_out": ((queries, wide), BF16)}
    dma = lambda count: pltpu.SemaphoreType.DMA((max(count, 1),))
    scratch = {name + "_v": pltpu.VMEM(a.shape, a.dtype) for name, a in streamed.items()}
    scratch |= {
        "load": dma(3),
        "grad_n": pltpu.VMEM((tokens, width), BF16),
        "resid_n": pltpu.VMEM((tokens, width), BF16),
        "feat": pltpu.VMEM((tokens, width), BF16),
        "osend": pltpu.VMEM((chips, queries, wide), BF16),
        "orecv": pltpu.VMEM((chips, queries, wide), BF16),
        "own": pltpu.VMEM((chips, queries, wide), F32),
        "o2send": pltpu.VMEM((max(chips - 1, 1), queries, wide), BF16),
        "o2recv": pltpu.VMEM((max(chips - 1, 1), queries, wide), BF16),
    }
    middle = -(-width // 256) * 128
    spans = [(0, middle), (middle, width)]
    sems = {"feat": 1, "pair": chips, "out": chips - 1}
    if fused:
        outs["proj_grad"] = ((rows, width), F32)
        scratch |= {
            "dwf": pltpu.VMEM((n, rows, width), F32),
            "dwb": pltpu.VMEM((m, rows, width), BF16),
            "xrecv": pltpu.VMEM((m, rows, width), BF16),
            "zsend": pltpu.VMEM((max(m - 1, 1), rows, width), BF16),
            "zrecv": pltpu.VMEM((max(m - 1, 1), rows, width), BF16),
        }
        sems |= {"rs_x": m, "rs_z": m - 1}
    for i, (lo, hi) in enumerate(spans):
        scratch |= {
            f"hs{i}": pltpu.VMEM((2, half, hi - lo), F32),
            f"crecv{i}": pltpu.VMEM((half, hi - lo), F32),
            f"ysend{i}": pltpu.VMEM((half, hi - lo), BF16),
            f"yrecv{i}": pltpu.VMEM((max(chips - 1, 1), half, hi - lo), BF16),
        }
        sems |= {f"core{i}": 1, f"y{i}": chips - 1}
        if fused:
            scratch[f"gath{i}"] = pltpu.VMEM((n, rows, hi - lo), BF16)
            sems |= {f"ag_z{i}": m - 1, f"ag_x{i}": m}
    for name, count in sems.items():
        scratch |= {name + "_s": dma(count), name + "_r": dma(count)}

    names = list(ins) + list(streamed) + list(outs) + list(scratch)
    vmem = pl.BlockSpec(memory_space=pltpu.VMEM)
    results = pl.pallas_call(
        functools.partial(kernel, names, n, h, fused, spans),
        out_shape=[jax.ShapeDtypeStruct(*v) for v in outs.values()],
        in_specs=[vmem] * len(ins) + [pl.BlockSpec(memory_space=pl.ANY)] * len(streamed),
        out_specs=[vmem] * len(outs),
        scratch_shapes=list(scratch.values()),
        compiler_params=pltpu.CompilerParams(collective_id=0, has_side_effects=True),
    )(*ins.values(), *streamed.values())
    results = pl.pallas_call(
        hand_over,
        out_shape=[jax.ShapeDtypeStruct(*v) for v in outs.values()],
        in_specs=[vmem] * len(outs),
        out_specs=[vmem] * len(outs),
    )(*results)
    results = dict(zip(outs, results))
    if fused:
        proj_grad = results["proj_grad"]
    else:
        proj_grad = lax.psum_scatter(
            lax.dot_general(vit_ctx, vit_grad, (((0,), (0,)), ((), ())), preferred_element_type=F32),
            "dp", scatter_dimension=0, tiled=True,
        )
    return (results["ctx_grad"], proj_grad[None], results["cross_out"][None])


def solution(mesh):
    return jax.shard_map(
        functools.partial(on_device, mesh.shape["dp"], mesh.shape["head"]),
        mesh=mesh,
        in_specs=(
            P("dp", "head"),
            P("dp", None),
            P("head", "dp", None),
            P("dp", None),
            P(),
            P(None, "head"),
            P(None, "head"),
            P(None, "head"),
            P("head", None),
            P(None, "head"),
        ),
        out_specs=(P("dp", "head"), P("head", "dp", None), P("dp", None, "head")),
        check_vma=False,
    )
```

```python
import functools
import math

import jax
import jax.numpy as jnp
from jax import lax
from jax.experimental import pallas as pl
from jax.experimental.pallas import tpu as pltpu
from jax.sharding import PartitionSpec as P

HD = 128
EPSILON = 1e-06
MESH = pl.DeviceIdType.MESH
F32 = jnp.float32
BF16 = jnp.bfloat16


def peer_along(at, step, count):
    if count & (count - 1):
        return lax.rem(at + step, count)
    bit = 1
    while bit < count:
        if step & bit:
            at = at + bit - 2 * bit * lax.rem(at // bit, 2)
        bit *= 2
    return at


def kernel(names, n, h, fused, spans, streams, *refs):
    r = dict(zip(names, refs), spans=spans, streams=streams)
    ctx, resid, grad, gain, cross_q, query_state = (
        r[k + "_v"] for k in ("ctx", "resid", "grad", "gain", "cross_q", "query_state")
    )
    proj = r["proj"]
    d, e = lax.axis_index("dp"), lax.axis_index("head")
    m, chips = n // 2, h // 2
    z, x = d // 2, lax.rem(d, 2)
    y, c = e // 2, lax.rem(e, 2)
    x_peer = (2 * z + 1 - x, e)
    z_pos = [z] + [peer_along(z, k, m) for k in range(1, m)] if fused else []
    z_peer = [(2 * p + x, e) for p in z_pos]
    core_peer = (d, 2 * y + 1 - c)
    y_pos = [y] + [lax.rem(y + k, chips) for k in range(1, chips)]
    y_peer = [(d, 2 * p + c) for p in y_pos]

    def remote(src, dst, name, at, device):
        copy = pltpu.make_async_remote_copy(
            src_ref=src,
            dst_ref=dst,
            send_sem=r[name + "_s"].at[at],
            recv_sem=r[name + "_r"].at[at],
            device_id=device,
            device_id_type=MESH,
        )
        copy.start()
        return copy

    loads = []
    for i, name in enumerate(r["streams"]):
        load = pltpu.make_async_copy(r[name], r[name + "_v"], r["load"].at[i])
        load.start()
        loads.append(load)
    waits = dict(zip(r["streams"], loads))

    greet = ([x_peer] + z_peer[1:] if fused else []) + [core_peer] + y_peer[1:]
    barrier = pltpu.get_barrier_semaphore()
    for device in greet:
        pl.semaphore_signal(barrier, inc=1, device_id=device, device_id_type=MESH)
    pl.semaphore_wait(barrier, len(greet))

    spans = r["spans"]
    width = spans[-1][1]

    def flip(src, dst):
        for lo in range(0, width, 128):
            hi = min(lo + 128, width)
            dst[:, lo:hi] = src[lo:hi, :].T

    if fused:
        rows = proj.shape[0]
        dwf, dwb = r["dwf"], r["dwb"]
        ag_z, ag_x = {}, {}
        for i, (lo, hi) in enumerate(spans):
            piece, gath = proj.at[:, lo:hi], r[f"gath{i}"]
            ag_x[i, 0] = remote(piece, gath.at[d], f"ag_x{i}", 0, x_peer)
            for k in range(1, m):
                ag_z[i, k] = remote(piece, gath.at[d], f"ag_z{i}", k - 1, z_peer[k])
            gath[d] = piece[...]
        waits["ctx"].wait()
        waits["grad"].wait()
        ctx_t = ctx[...].T
        for lo in range(0, width, 256):
            hi = min(lo + 256, width)
            part = lax.dot_general(
                ctx_t, grad[lo:hi, :], (((1,), (1,)), ((), ())), preferred_element_type=F32
            )
            dwf[:, :, lo:hi] = part.reshape(n, rows, hi - lo)
        for k in range(m):
            dwb[k] = dwf[2 * z_pos[k] + 1 - x].astype(BF16)
        early = [m - 1]
        rs_x = {k: remote(dwb.at[k], r["xrecv"].at[k], "rs_x", k, x_peer) for k in early}
    else:
        rs_x = {}
        waits["ctx"].wait()
        waits["grad"].wait()
    flip(grad, r["grad_n"])
    waits["resid"].wait()
    flip(resid, r["resid_n"])
    grad, resid = r["grad_n"], r["resid_n"]

    half = ctx.shape[0] // 2
    own_rows = pl.ds(pl.multiple_of(c * half, half), half)
    peer_rows = pl.ds(pl.multiple_of((1 - c) * half, half), half)
    feat = r["feat"]
    to_core, to_y, rs_z = {}, {}, {}

    def forward(i, k):
        ag_z[i, k].wait_recv()
        here = r[f"gath{i}"].at[2 * z_pos[k] + x]
        ag_x[i, k] = remote(here, here, f"ag_x{i}", k, x_peer)

    def matrix(i):
        lo, hi = spans[i]
        return r[f"gath{i}"][...].reshape(n * rows, hi - lo) if fused else proj[:, lo:hi]

    def product(i):
        if fused:
            for k in range(m):
                ag_x[i, k].wait_recv()
        hs = r[f"hs{i}"]
        hs[1] = jnp.dot(ctx[peer_rows, :], matrix(i), preferred_element_type=F32)
        to_core[i] = remote(hs.at[1], r[f"crecv{i}"], f"core{i}", 0, core_peer)
        hs[0] = jnp.dot(ctx[own_rows, :], matrix(i), preferred_element_type=F32)

    def exchange(i):
        hs, ysend, yrecv = r[f"hs{i}"], r[f"ysend{i}"], r[f"yrecv{i}"]
        to_core[i].wait_recv()
        chip_sum = hs[0] + r[f"crecv{i}"][...]
        hs[0] = chip_sum
        ysend[...] = chip_sum.astype(BF16)
        for k in range(1, chips):
            to_y[i, k] = remote(ysend, yrecv.at[k - 1], f"y{i}", k - 1, y_peer[k])

    def pass_on(k):
        rs_x[k].wait_recv()
        r["zsend"][k - 1] = (dwf[2 * z_pos[k] + x] + r["xrecv"][k].astype(F32)).astype(BF16)
        rs_z[k] = remote(r["zsend"].at[k - 1], r["zrecv"].at[k - 1], "rs_z", k - 1, z_peer[k])

    todo = list(range(m - 1, 0, -1)) if fused else []
    last = len(spans) - 1
    for i in range(len(spans)):
        steps = list(range(1, m)) if fused else []
        if i == 0:
            for k in steps:
                forward(i, k)
        ahead = steps if i < last else []
        for k in ahead[:1]:
            forward(i + 1, k)
        product(i)
        for k in ahead[1:2]:
            forward(i + 1, k)
        exchange(i)
        for k in ahead[2:]:
            forward(i + 1, k)
        if fused and i == max(last - 1, 0):
            for k in [k for k in todo + [0] if k not in rs_x]:
                rs_x[k] = remote(dwb.at[k], r["xrecv"].at[k], "rs_x", k, x_peer)
            for _ in todo[:1]:
                pass_on(todo.pop(0))

    grads = 0.0
    for i, (lo, hi) in enumerate(spans):
        grads = grads + lax.dot_general(
            grad[:, lo:hi], matrix(i), (((1,), (1,)), ((), ())), preferred_element_type=F32
        )
    r["ctx_grad"][...] = grads.astype(BF16)
    if todo:
        pass_on(todo.pop(0))

    total, squares = 0.0, 0.0
    for i, (lo, hi) in enumerate(spans):
        hidden = resid[own_rows, lo:hi].astype(F32) + r[f"hs{i}"][0]
        for k in range(1, chips):
            to_y[i, k].wait_recv()
            hidden = hidden + r[f"yrecv{i}"][k - 1].astype(F32)
        r[f"hs{i}"][0] = hidden
        total = total + jnp.sum(hidden, axis=1, keepdims=True)
        squares = squares + jnp.sum(hidden * hidden, axis=1, keepdims=True)
    row_mean, square_mean = total / width, squares / width
    variance = square_mean - row_mean * row_mean
    inverse = lax.rsqrt(variance + EPSILON)
    waits["gain"].wait()
    scales = gain[...].reshape(1, width)
    for i, (lo, hi) in enumerate(spans):
        feat[own_rows, lo:hi] = (
            (r[f"hs{i}"][0] - row_mean) * inverse * scales[:, lo:hi]
        ).astype(BF16)
    to_feat = remote(feat.at[own_rows], feat.at[own_rows], "feat", 0, core_peer)
    if len(todo) > 1:
        pass_on(todo.pop(0))
    for name in ("key_w", "value_w", "cross_q"):
        waits[name].wait()
    to_feat.wait_recv()

    rows_of = feat[...]
    keys = jnp.dot(rows_of, r["key_w_v"][...], preferred_element_type=F32).astype(BF16)
    values = jnp.dot(rows_of, r["value_w_v"][...], preferred_element_type=F32).astype(BF16)
    while todo:
        pass_on(todo.pop(0))
    scale = 1.0 / math.sqrt(HD)
    attended = []
    for lo in range(0, keys.shape[1], HD):
        scores = (
            lax.dot_general(
                cross_q[:, lo : lo + HD],
                keys[:, lo : lo + HD],
                (((1,), (1,)), ((), ())),
                preferred_element_type=F32,
            )
            * scale
        )
        exponent = jnp.exp(scores - jnp.max(scores, axis=1, keepdims=True))
        probs = (exponent / jnp.sum(exponent, axis=1, keepdims=True)).astype(BF16)
        attended.append(
            jnp.dot(probs, values[:, lo : lo + HD], preferred_element_type=F32).astype(BF16)
        )
    attended = jnp.concatenate(attended, axis=1)

    waits["out_w"].wait()
    waits["query_state"].wait()
    out_w, wide = r["out_w_v"], query_state.shape[1]

    def term(chip, core):
        at = pl.multiple_of((2 * chip + core) * wide, 128)
        return jnp.dot(attended, out_w[:, pl.ds(at, wide)], preferred_element_type=F32)

    osend, orecv, own = r["osend"], r["orecv"], r["own"]
    to_pair, to_out = {}, {}
    order = list(range(1, chips)) + [0]
    for k in order:
        osend[k] = term(y_pos[k], 1 - c).astype(BF16)
        to_pair[k] = remote(osend.at[k], orecv.at[k], "pair", k, core_peer)
        own[k] = term(y_pos[k], c)
        if k:
            to_pair[k].wait_recv()
            r["o2send"][k - 1] = (own[k] + orecv[k].astype(F32)).astype(BF16)
            to_out[k] = remote(r["o2send"].at[k - 1], r["o2recv"].at[k - 1], "out", k - 1, y_peer[k])

    while todo:
        pass_on(todo.pop(0))
    if fused:
        rs_x[0].wait_recv()
        total = dwf[d] + r["xrecv"][0].astype(F32)
        for k in range(m - 1, 0, -1):
            rs_z[k].wait_recv()
            total = total + r["zrecv"][k - 1].astype(F32)
        r["proj_grad"][...] = total

    to_pair[0].wait_recv()
    result = query_state[...].astype(F32) + own[0] + orecv[0].astype(F32)
    for k in range(1, chips):
        to_out[k].wait_recv()
        result = result + r["o2recv"][k - 1].astype(F32)
    r["cross_out"][...] = result.astype(BF16)

    groups = [to_core, to_y, to_pair, to_out] + ([ag_z, ag_x, rs_x, rs_z] if fused else [])
    sends = [to_feat] + [copy for group in groups for copy in group.values()]
    for copy in sends:
        copy.wait_send()


def hand_over(*refs):
    count = len(refs) // 2
    for src, dst in zip(refs[:count], refs[count:]):
        dst[...] = src[...]


def on_device(
    n, h, vit_ctx, vit_resid, vit_proj, vit_grad, norm_gain, cross_q, key_w, value_w, out_w, query_state
):
    rows, width = vit_proj.shape[1:]
    fused = rows % 16 == 0 and n % 2 == 0
    tokens, vrows = vit_ctx.shape
    queries, wide = query_state.shape
    m, chips, half = n // 2, h // 2, tokens // 2
    proj = vit_proj[0] if fused else lax.all_gather(vit_proj, "dp", axis=1, tiled=True)[0]

    ins = {"proj": proj}
    streamed = {
        "ctx": vit_ctx, "grad": vit_grad.T, "resid": vit_resid.T, "key_w": key_w, "value_w": value_w,
        "gain": norm_gain, "cross_q": cross_q, "query_state": query_state, "out_w": out_w,
    }
    outs = {"ctx_grad": ((tokens, vrows), BF16), "cross_out": ((queries, wide), BF16)}
    dma = lambda count: pltpu.SemaphoreType.DMA((max(count, 1),))
    scratch = {name + "_v": pltpu.VMEM(a.shape, a.dtype) for name, a in streamed.items()}
    scratch |= {
        "load": dma(len(streamed)),
        "grad_n": pltpu.VMEM((tokens, width), BF16),
        "resid_n": pltpu.VMEM((tokens, width), BF16),
        "feat": pltpu.VMEM((tokens, width), BF16),
        "osend": pltpu.VMEM((chips, queries, wide), BF16),
        "orecv": pltpu.VMEM((chips, queries, wide), BF16),
        "own": pltpu.VMEM((chips, queries, wide), F32),
        "o2send": pltpu.VMEM((max(chips - 1, 1), queries, wide), BF16),
        "o2recv": pltpu.VMEM((max(chips - 1, 1), queries, wide), BF16),
    }
    middle = -(-width // 256) * 128
    spans = [(0, middle), (middle, width)]
    sems = {"feat": 1, "pair": chips, "out": chips - 1}
    if fused:
        outs["proj_grad"] = ((rows, width), F32)
        scratch |= {
            "dwf": pltpu.VMEM((n, rows, width), F32),
            "dwb": pltpu.VMEM((m, rows, width), BF16),
            "xrecv": pltpu.VMEM((m, rows, width), BF16),
            "zsend": pltpu.VMEM((max(m - 1, 1), rows, width), BF16),
            "zrecv": pltpu.VMEM((max(m - 1, 1), rows, width), BF16),
        }
        sems |= {"rs_x": m, "rs_z": m - 1}
    for i, (lo, hi) in enumerate(spans):
        scratch |= {
            f"hs{i}": pltpu.VMEM((2, half, hi - lo), F32),
            f"crecv{i}": pltpu.VMEM((half, hi - lo), F32),
            f"ysend{i}": pltpu.VMEM((half, hi - lo), BF16),
            f"yrecv{i}": pltpu.VMEM((max(chips - 1, 1), half, hi - lo), BF16),
        }
        sems |= {f"core{i}": 1, f"y{i}": chips - 1}
        if fused:
            scratch[f"gath{i}"] = pltpu.VMEM((n, rows, hi - lo), BF16)
            sems |= {f"ag_z{i}": m - 1, f"ag_x{i}": m}
    for name, count in sems.items():
        scratch |= {name + "_s": dma(count), name + "_r": dma(count)}

    names = list(ins) + list(streamed) + list(outs) + list(scratch)
    vmem = pl.BlockSpec(memory_space=pltpu.VMEM)
    results = pl.pallas_call(
        functools.partial(kernel, names, n, h, fused, spans, list(streamed)),
        out_shape=[jax.ShapeDtypeStruct(*v) for v in outs.values()],
        in_specs=[vmem] * len(ins) + [pl.BlockSpec(memory_space=pl.ANY)] * len(streamed),
        out_specs=[vmem] * len(outs),
        scratch_shapes=list(scratch.values()),
        compiler_params=pltpu.CompilerParams(collective_id=0, has_side_effects=True),
    )(*ins.values(), *streamed.values())
    results = pl.pallas_call(
        hand_over,
        out_shape=[jax.ShapeDtypeStruct(*v) for v in outs.values()],
        in_specs=[vmem] * len(outs),
        out_specs=[vmem] * len(outs),
    )(*results)
    results = dict(zip(outs, results))
    if fused:
        proj_grad = results["proj_grad"]
    else:
        proj_grad = lax.psum_scatter(
            lax.dot_general(vit_ctx, vit_grad, (((0,), (0,)), ((), ())), preferred_element_type=F32),
            "dp", scatter_dimension=0, tiled=True,
        )
    return (results["ctx_grad"], proj_grad[None], results["cross_out"][None])


def solution(mesh):
    return jax.shard_map(
        functools.partial(on_device, mesh.shape["dp"], mesh.shape["head"]),
        mesh=mesh,
        in_specs=(
            P("dp", "head"),
            P("dp", None),
            P("head", "dp", None),
            P("dp", None),
            P(),
            P(None, "head"),
            P(None, "head"),
            P(None, "head"),
            P("head", None),
            P(None, "head"),
        ),
        out_specs=(P("dp", "head"), P("head", "dp", None), P("dp", None, "head")),
        check_vma=False,
    )
```
